256 devices in a mesh: src: 32 (over z, y_lo, core), tgt: 8 (over y_hi, x).
Axes of the slice: x: 4, y: 4 (y_hi: 2, y_lo: 2; y = y_hi * 2 + y_lo), z: 8, core: 2. Of those that a mesh axis runs over, the one named last changes fastest.
Arguments:
- inputs: bfloat16 [512, 2, 1024, 512], P(('src', 'tgt')), may hold values from -6 to 6
- leaf_maps: bfloat16 [512, 2, 256, 1024], P(('src', 'tgt')), may hold values from -0.125 to 0.125
- transfer_blocks: bfloat16 [4, 512, 2, 2, 256, 256], P(None, ('src', 'tgt')), may hold values from -0.1875 to 0.1875
Outputs:
- butterfly_out: bfloat16 [512, 2, 256, 512], P(('src', 'tgt'))
The draws below stay inside these ranges and needn't reach their ends.
All inputs are finite; a program needn't handle non-finite values.
Results may differ from the reference program's by a relative error of at most 0.012.
Values may be sent and summed in bfloat16 or wider, within the bound.
No kernel may reach another device: no remote copies, remote signals or barrier semaphores. Data moves between devices by JAX's collectives and lax.ppermute only.
A program may use at most 64 MiB of HBM per device.

```python
import jax
import jax.numpy as jnp
from jax import lax

M = 1024
K = 256
R = 512
LEVELS = 4
LEAVES = 512
N_TGT = 8


def level_of(rng, extent, shards, smallest, high):
    def one(position, shards_of):
        heights = jax.random.uniform(jax.random.fold_in(jax.random.fold_in(rng, 6), position), (shards_of,), jnp.float32, smallest / len(shards), high / len(shards))
        return jnp.repeat(jnp.exp(heights), extent[position] // shards_of).reshape((-1,) + (1,) * (len(extent) - position - 1))

    factor_of = one(*shards[0])
    for cut in shards[1:]:
        factor_of = factor_of * one(*cut)
    return factor_of


def normal_values(rng, shape, deviation, bound, split=(), kind=jnp.bfloat16):
    level = level_of(rng, shape, split, -0.22, 0.18) if split else 1.0
    entries = jax.random.normal(rng, shape, jnp.float32) * deviation * level
    return jnp.minimum(jnp.maximum(entries, -bound), bound).astype(kind)


def setup_inputs(seed: int = 0) -> dict:
    seeds = jax.random.split(jax.random.key(seed), 4)
    return {
        "inputs": normal_values(seeds[0], (LEAVES, 2, M, R), 1.0, 6.0, ((0, 256),)),
        "leaf_maps": normal_values(seeds[1], (LEAVES, 2, K, M), (2 * M) ** -0.5, 0.125, ((0, 256),)),
        "transfer_blocks": normal_values(seeds[2], (LEVELS, LEAVES, 2, 2, K, K), (4 * K) ** -0.5, 0.1875, ((1, 256),)),
    }


def complex_product(blocks, vectors):
    real_part = jnp.dot(blocks[0], vectors[0], preferred_element_type=jnp.float32) - jnp.dot(blocks[1], vectors[1], preferred_element_type=jnp.float32)
    imag_part = jnp.dot(blocks[0], vectors[1], preferred_element_type=jnp.float32) + jnp.dot(blocks[1], vectors[0], preferred_element_type=jnp.float32)
    return jnp.stack([real_part, imag_part])


def butterfly_level(coeffs, blocks, stride):
    groups = LEAVES // (2 * stride)
    paired = coeffs.reshape(groups, 2, stride, 2, K, R).transpose(0, 2, 1, 3, 4, 5).reshape(groups * stride, 2, 2, K, R)
    block_pairs = blocks.reshape(groups, 2, stride, 2, 2, K, K).transpose(0, 2, 1, 3, 4, 5, 6).reshape(groups * stride, 2, 2, 2, K, K)

    def combine_pair(pair_items):
        vectors, pair_blocks = pair_items
        halves = []
        for target_bit in range(2):
            own_term = complex_product(pair_blocks[target_bit, target_bit], vectors[target_bit])
            partner = complex_product(pair_blocks[1 - target_bit, target_bit], vectors[1 - target_bit]).astype(jnp.bfloat16)
            halves.append(own_term + partner.astype(jnp.float32))
        return jnp.stack(halves).astype(jnp.bfloat16)

    updated = lax.map(combine_pair, (paired, block_pairs))
    return updated.reshape(groups, stride, 2, 2, K, R).transpose(0, 2, 1, 3, 4, 5).reshape(LEAVES, 2, K, R)


def reference(inputs, leaf_maps, transfer_blocks):
    coeffs = lax.map(lambda pair_items: complex_product(pair_items[0], pair_items[1]).astype(jnp.bfloat16), (leaf_maps, inputs))
    for level_index, stride in enumerate((1, LEAVES // 2, LEAVES // 4, N_TGT)):
        coeffs = butterfly_level(coeffs, transfer_blocks[level_index], stride)
    return coeffs
```

```python
import functools

import jax
import jax.numpy as jnp
from jax import lax
from jax.experimental import pallas as pl
from jax.experimental.pallas import tpu as pltpu
from jax.sharding import PartitionSpec as P

CHUNKS = 4
VMEM_LIMIT = 40 * 1024 * 1024


def partner_2(block, axis, apart):
    count = lax.axis_size(axis)
    route = []
    for low in range(count):
        high = low | 1 << apart
        if high != low and high < count:
            route += [(low, high), (high, low)]
    return lax.ppermute(block, axis, route)


def own_bit(axis, place):
    return lax.rem(lax.div(lax.axis_index(axis), 2**place), 2)


def product(blocks, vectors):
    stacked = vectors.reshape(2 * vectors.shape[1], vectors.shape[2])
    real_rows = jnp.concatenate([blocks[0], -blocks[1]], axis=1)
    imag_rows = jnp.concatenate([blocks[1], blocks[0]], axis=1)
    real_part = jnp.dot(real_rows, stacked, preferred_element_type=jnp.float32)
    imag_part = jnp.dot(imag_rows, stacked, preferred_element_type=jnp.float32)
    return jnp.stack([real_part, imag_part])


def first_kernel(chunk, width, place, x_hbm, l_hbm, t_hbm, a_ref, p_ref, x, l, t0, t1, sems):
    other = 1 - own_bit(*place)
    columns = pl.ds(chunk * width, width)
    moves = []
    for b in range(2):
        moves.append(pltpu.make_async_copy(l_hbm.at[b], l.at[b], sems.at[b]))
        moves.append(pltpu.make_async_copy(x_hbm.at[b, :, :, columns], x.at[b], sems.at[2 + b]))
    moves.append(pltpu.make_async_copy(t_hbm.at[0], t0, sems.at[4]))
    moves.append(pltpu.make_async_copy(t_hbm.at[1, :, other], t1, sems.at[5]))
    for move in moves:
        move.start()
    coeffs = []
    for b in range(2):
        moves[2 * b].wait()
        moves[2 * b + 1].wait()
        coeffs.append(product(l[b], x[b]).astype(jnp.bfloat16))
    moves[4].wait()
    after = []
    for b in range(2):
        own_term = product(t0[b, b], coeffs[b])
        partner = product(t0[1 - b, b], coeffs[1 - b]).astype(jnp.bfloat16)
        after.append((own_term + partner.astype(jnp.float32)).astype(jnp.bfloat16))
        a_ref[b] = after[b]
    moves[5].wait()
    for b in range(2):
        p_ref[b] = product(t1[b], after[b]).astype(jnp.bfloat16)


def middle_kernel(level, place, next_place, a_ref, in_ref, t_hbm, a_out, p_out, kept, send, sems):
    own = own_bit(*place)
    other = 1 - own_bit(*next_place)
    moves = [
        pltpu.make_async_copy(t_hbm.at[level, :, own], kept, sems.at[0]),
        pltpu.make_async_copy(t_hbm.at[level + 1, :, other], send, sems.at[1]),
    ]
    for move in moves:
        move.start()
    moves[0].wait()
    after = []
    for b in range(2):
        own_term = product(kept[b], a_ref[b])
        after.append((own_term + in_ref[b].astype(jnp.float32)).astype(jnp.bfloat16))
        a_out[b] = after[b]
    moves[1].wait()
    for b in range(2):
        p_out[b] = product(send[b], after[b]).astype(jnp.bfloat16)


def last_kernel(level, chunk, width, place, a_ref, in_ref, t_hbm, *refs):
    out_hbm, kept, out, sems = refs[-4:]
    own = own_bit(*place)
    move = pltpu.make_async_copy(t_hbm.at[level, :, own], kept, sems.at[0])
    move.start()
    move.wait()
    for b in range(2):
        own_term = product(kept[b], a_ref[b])
        out[b] = (own_term + in_ref[b].astype(jnp.float32)).astype(jnp.bfloat16)
    store = pltpu.make_async_copy(out, out_hbm.at[:, :, :, pl.ds(chunk * width, width)], sems.at[1])
    store.start()
    store.wait()


def local(inputs, leaf_maps, transfer_blocks):
    nodes, _, rank, rows = leaf_maps.shape
    columns = inputs.shape[3]
    width = columns // CHUNKS
    src_bits = lax.axis_size("src").bit_length() - 1
    tgt_bits = lax.axis_size("tgt").bit_length() - 1
    places = [None, ("src", src_bits - 1), ("src", src_bits - 2), ("tgt", tgt_bits - 1)]

    part = jax.ShapeDtypeStruct((nodes, 2, rank, width), jnp.bfloat16)
    anywhere = pl.BlockSpec(memory_space=pltpu.HBM)
    here = pl.BlockSpec(memory_space=pltpu.VMEM)
    params = pltpu.CompilerParams(vmem_limit_bytes=VMEM_LIMIT)
    one_product = 8 * rank * rank * width * nodes
    half_level = pltpu.VMEM((nodes, 2, rank, rank), jnp.bfloat16)

    def first(chunk):
        return pl.pallas_call(
            functools.partial(first_kernel, chunk, width, places[1]),
            out_shape=(part, part),
            in_specs=[anywhere] * 3,
            out_specs=(here, here),
            scratch_shapes=[
                pltpu.VMEM((nodes, 2, rows, width), jnp.bfloat16),
                pltpu.VMEM((nodes, 2, rank, rows), jnp.bfloat16),
                pltpu.VMEM((nodes, 2, 2, rank, rank), jnp.bfloat16),
                half_level,
                pltpu.SemaphoreType.DMA((6,)),
            ],
            compiler_params=params,
            cost_estimate=pl.CostEstimate(
                flops=one_product * (rows // rank + 3), bytes_accessed=5 * 2**20, transcendentals=0
            ),
            name="first",
        )(inputs, leaf_maps, transfer_blocks)

    def middle(level, held, arrived):
        return pl.pallas_call(
            functools.partial(middle_kernel, level, places[level], places[level + 1]),
            out_shape=(part, part),
            in_specs=[here, here, anywhere],
            out_specs=(here, here),
            scratch_shapes=[half_level, half_level, pltpu.SemaphoreType.DMA((2,))],
            compiler_params=params,
            cost_estimate=pl.CostEstimate(
                flops=one_product * 2, bytes_accessed=2 * 2**20, transcendentals=0
            ),
            name="middle",
        )(held, arrived, transfer_blocks)

    def last(level, chunk, held, arrived, result):
        operands = (held, arrived, transfer_blocks)
        aliases = {}
        if result is not None:
            operands += (result,)
            aliases = {3: 0}
        return pl.pallas_call(
            functools.partial(last_kernel, level, chunk, width, places[level]),
            out_shape=jax.ShapeDtypeStruct((nodes, 2, rank, columns), jnp.bfloat16),
            in_specs=[here, here, anywhere] + [anywhere] * len(aliases),
            out_specs=anywhere,
            scratch_shapes=[
                half_level,
                pltpu.VMEM((nodes, 2, rank, width), jnp.bfloat16),
                pltpu.SemaphoreType.DMA((2,)),
            ],
            input_output_aliases=aliases,
            compiler_params=params,
            cost_estimate=pl.CostEstimate(
                flops=one_product, bytes_accessed=2**20, transcendentals=0
            ),
            name="last",
        )(*operands)

    held = [None] * CHUNKS
    flying = [None] * CHUNKS
    for chunk in range(CHUNKS):
        held[chunk], term = first(chunk)
        flying[chunk] = partner_2(term, *places[1])
    for level in (1, 2):
        for chunk in range(CHUNKS):
            held[chunk], term = middle(level, held[chunk], flying[chunk])
            flying[chunk] = partner_2(term, *places[level + 1])
    result = None
    for chunk in range(CHUNKS):
        result = last(3, chunk, held[chunk], flying[chunk], result)
    return result


def solution(mesh):
    placed = (
        P(("src", "tgt"), None, None, None),
        P(("src", "tgt"), None, None, None),
        P(None, ("src", "tgt"), None, None, None, None),
    )
    return jax.shard_map(
        local,
        mesh=mesh,
        in_specs=placed,
        out_specs=P(("src", "tgt"), None, None, None),
        check_vma=False,
    )
```

```python
import functools

import jax
import jax.numpy as jnp
from jax import lax
from jax.experimental import pallas as pl
from jax.experimental.pallas import tpu as pltpu
from jax.sharding import PartitionSpec as P

HALVES = 2
PIECES = 4
FIRST_LIMIT = 62 * 1024 * 1024
SECOND_LIMIT = 54 * 1024 * 1024
LIMIT = 32 * 1024 * 1024


def partner_2(block, axis, apart):
    count = lax.axis_size(axis)
    route = []
    for low in range(count):
        high = low | 1 << apart
        if high != low and high < count:
            route += [(low, high), (high, low)]
    return lax.ppermute(block, axis, route)


def own_bit(axis, place):
    return lax.rem(lax.div(lax.axis_index(axis), 2**place), 2)


def product(blocks, vectors):
    stacked = vectors.reshape(2 * vectors.shape[1], vectors.shape[2])
    real_rows = jnp.concatenate([blocks[0], -blocks[1]], axis=1)
    imag_rows = jnp.concatenate([blocks[1], blocks[0]], axis=1)
    rows = jnp.concatenate([real_rows, imag_rows], axis=0)
    both = jnp.dot(rows, stacked, preferred_element_type=jnp.float32)
    return both.reshape(2, blocks.shape[1], vectors.shape[2])


def first_pair(target, t0, coeffs):
    own_term = product(t0[target, target], coeffs[target])
    partner = product(t0[1 - target, target], coeffs[1 - target]).astype(jnp.bfloat16)
    return (own_term + partner.astype(jnp.float32)).astype(jnp.bfloat16)


def leaf_kernel(
    start, width, place, x_hbm, l_hbm, t_hbm, a0_ref, a1_ref, p0_ref, p1_ref, x, l, t0, t1, sems
):
    other = 1 - own_bit(*place)
    columns = pl.ds(start, width)
    deep = l_hbm.shape[3] // PIECES
    nodes = l_hbm.shape[0]
    moves = []
    for b in range(nodes):
        for piece in range(PIECES):
            span = pl.ds(piece * deep, deep)
            place_at = b * PIECES + piece
            moves.append(
                (
                    pltpu.make_async_copy(
                        l_hbm.at[b, :, :, span], l.at[b, :, :, span], sems.at[2 * place_at]
                    ),
                    pltpu.make_async_copy(
                        x_hbm.at[b, :, span, columns], x.at[b, :, span], sems.at[2 * place_at + 1]
                    ),
                )
            )
    base = 2 * nodes * PIECES
    blocks_0 = pltpu.make_async_copy(t_hbm.at[0], t0, sems.at[base])
    blocks_1 = pltpu.make_async_copy(t_hbm.at[1, :, other], t1, sems.at[base + 1])
    for pair in moves:
        for move in pair:
            move.start()
    blocks_0.start()
    blocks_1.start()
    coeffs = []
    for b in range(nodes):
        total = None
        for piece in range(PIECES):
            for move in moves[b * PIECES + piece]:
                move.wait()
            span = slice(piece * deep, (piece + 1) * deep)
            term = product(l[b, :, :, span], x[b, :, span, :])
            total = term if total is None else total + term
        coeffs.append(total.astype(jnp.bfloat16))
    blocks_0.wait()
    for b, (a_ref, p_ref) in enumerate(((a0_ref, p0_ref), (a1_ref, p1_ref))):
        after = first_pair(b, t0, coeffs)
        a_ref[...] = after
        if b == 0:
            blocks_1.wait()
        p_ref[...] = product(t1[b], after).astype(jnp.bfloat16)


def middle_kernel(level, node, place, next_place, a_ref, in_ref, t_ref, a_out, p_out):
    own = own_bit(*place)
    other = 1 - own_bit(*next_place)
    own_term = product(t_ref[level, node, own], a_ref[...])
    after = (own_term + in_ref[...].astype(jnp.float32)).astype(jnp.bfloat16)
    a_out[...] = after
    p_out[...] = product(t_ref[level + 1, node, other], after).astype(jnp.bfloat16)


def last_kernel(level, node, start, width, place, a_ref, in_ref, t_ref, *refs):
    out_hbm, out, sems = refs[-3:]
    own = own_bit(*place)
    own_term = product(t_ref[level, node, own], a_ref[...])
    out[...] = (own_term + in_ref[...].astype(jnp.float32)).astype(jnp.bfloat16)
    store = pltpu.make_async_copy(out, out_hbm.at[node, :, :, pl.ds(start, width)], sems.at[0])
    store.start()
    store.wait()


def local(inputs, leaf_maps, transfer_blocks):
    nodes, _, rank, rows = leaf_maps.shape
    columns = inputs.shape[3]
    width = columns // HALVES
    src_bits = lax.axis_size("src").bit_length() - 1
    tgt_bits = lax.axis_size("tgt").bit_length() - 1
    places = [None, ("src", src_bits - 1), ("src", src_bits - 2), ("tgt", tgt_bits - 1)]

    part = jax.ShapeDtypeStruct((2, rank, width), jnp.bfloat16)
    anywhere = pl.BlockSpec(memory_space=pltpu.HBM)
    here = pl.BlockSpec(memory_space=pltpu.VMEM)

    def params(limit):
        return pltpu.CompilerParams(vmem_limit_bytes=limit)

    def cost(products):
        return pl.CostEstimate(
            flops=products, bytes_accessed=products, transcendentals=0
        )

    def leaf(half):
        return pl.pallas_call(
            functools.partial(leaf_kernel, half * width, width, places[1]),
            out_shape=(part,) * 4,
            in_specs=[anywhere] * 3,
            out_specs=(here,) * 4,
            scratch_shapes=[
                pltpu.VMEM((nodes, 2, rows, width), jnp.bfloat16),
                pltpu.VMEM((nodes, 2, rank, rows), jnp.bfloat16),
                pltpu.VMEM((nodes, 2, 2, rank, rank), jnp.bfloat16),
                pltpu.VMEM((nodes, 2, rank, rank), jnp.bfloat16),
                pltpu.SemaphoreType.DMA((2 * nodes * PIECES + 2,)),
            ],
            compiler_params=params(FIRST_LIMIT if half == 0 else SECOND_LIMIT),
            cost_estimate=cost(nodes * (rows // rank + 3)),
            name="leaf",
        )(inputs, leaf_maps, transfer_blocks)

    def middle(level, node, held, arrived):
        return pl.pallas_call(
            functools.partial(middle_kernel, level, node, places[level], places[level + 1]),
            out_shape=(part, part),
            in_specs=[here] * 3,
            out_specs=(here, here),
            compiler_params=params(LIMIT),
            cost_estimate=cost(2),
            name="middle",
        )(held, arrived, transfer_blocks)

    def last(level, node, half, held, arrived, result):
        operands = (held, arrived, transfer_blocks)
        aliases = {}
        if result is not None:
            operands += (result,)
            aliases = {3: 0}
        return pl.pallas_call(
            functools.partial(last_kernel, level, node, half * width, width, places[level]),
            out_shape=jax.ShapeDtypeStruct((nodes, 2, rank, columns), jnp.bfloat16),
            in_specs=[here] * 3 + [anywhere] * len(aliases),
            out_specs=anywhere,
            scratch_shapes=[
                pltpu.VMEM((2, rank, width), jnp.bfloat16),
                pltpu.SemaphoreType.DMA((1,)),
            ],
            input_output_aliases=aliases,
            compiler_params=params(LIMIT),
            cost_estimate=cost(1),
            name="last",
        )(*operands)

    chunks = [(half, node) for half in range(HALVES) for node in range(nodes)]
    held, flying = {}, {}

    for half in range(HALVES):
        results = leaf(half)
        for node in range(nodes):
            held[half, node] = results[node]
            flying[half, node] = partner_2(results[nodes + node], *places[1])
    for level in (1, 2):
        for half, node in chunks:
            held[half, node], sent = middle(level, node, held[half, node], flying[half, node])
            flying[half, node] = partner_2(sent, *places[level + 1])
    result = None
    for half, node in chunks:
        result = last(3, node, half, held[half, node], flying[half, node], result)
    return result


def solution(mesh):
    placed = (
        P(("src", "tgt"), None, None, None),
        P(("src", "tgt"), None, None, None),
        P(None, ("src", "tgt"), None, None, None, None),
    )
    return jax.shard_map(
        local,
        mesh=mesh,
        in_specs=placed,
        out_specs=P(("src", "tgt"), None, None, None),
        check_vma=False,
    )
```

```python
import functools

import jax
import jax.numpy as jnp
from jax import lax
from jax.experimental import pallas as pl
from jax.experimental.pallas import tpu as pltpu
from jax.sharding import PartitionSpec as P

GROUPS = ((128, False), (128, False), (128, False), (128, False))
LEAF_LIMIT = 24 * 1024 * 1024
LIMIT = 16 * 1024 * 1024


def partner_2(block, axis, apart):
    count = lax.axis_size(axis)
    route = []
    for low in range(count):
        high = low | 1 << apart
        if high != low and high < count:
            route += [(low, high), (high, low)]
    return lax.ppermute(block, axis, route)


def own_bit(axis, place):
    return lax.rem(lax.div(lax.axis_index(axis), 2**place), 2)


def product(blocks, vectors):
    rank, width = blocks.shape[1], vectors.shape[2]
    if width >= 256:
        stacked = vectors.reshape(2 * vectors.shape[1], width)
        real_rows = jnp.concatenate([blocks[0], -blocks[1]], axis=1)
        imag_rows = jnp.concatenate([blocks[1], blocks[0]], axis=1)
        rows = jnp.concatenate([real_rows, imag_rows], axis=0)
        both = jnp.dot(rows, stacked, preferred_element_type=jnp.float32)
        return both.reshape(2, rank, width)
    rows = blocks.reshape(2 * rank, blocks.shape[2])
    beside = jnp.concatenate([vectors[0], vectors[1]], axis=1)
    all_four = jnp.dot(rows, beside, preferred_element_type=jnp.float32)
    real_part = all_four[:rank, :width] - all_four[rank:, width:]
    imag_part = all_four[:rank, width:] + all_four[rank:, :width]
    return jnp.stack([real_part, imag_part])


def leaf_kernel(start, width, apart, place, x_hbm, l_hbm, t_hbm, *refs):
    nodes = l_hbm.shape[0]
    outs, (x, l, t0, t1, sems) = refs[:-5], refs[-5:]
    if apart:
        a_refs, p_refs = [ref.at[0] for ref in outs[:nodes]], [ref.at[0] for ref in outs[nodes:]]
    else:
        a_refs, p_refs = [[ref.at[b] for b in range(nodes)] for ref in outs]
    other = 1 - own_bit(*place)
    columns = pl.ds(start, width)
    moves = []
    for b in range(nodes):
        moves.append(
            (
                pltpu.make_async_copy(x_hbm.at[b, :, :, columns], x.at[b], sems.at[2 * b]),
                pltpu.make_async_copy(l_hbm.at[b], l.at[b], sems.at[2 * b + 1]),
            )
        )
    blocks_0 = pltpu.make_async_copy(t_hbm.at[0], t0, sems.at[2 * nodes])
    blocks_1 = pltpu.make_async_copy(t_hbm.at[1, :, other], t1, sems.at[2 * nodes + 1])
    for pair in moves:
        for move in pair:
            move.start()
    blocks_0.start()
    blocks_1.start()
    coeffs = []
    for b in range(nodes):
        for move in moves[b]:
            move.wait()
        coeffs.append(product(l[b], x[b]).astype(jnp.bfloat16))
    blocks_0.wait()
    for b in range(nodes):
        own_term = product(t0[b, b], coeffs[b])
        partner = product(t0[1 - b, b], coeffs[1 - b]).astype(jnp.bfloat16)
        after = (own_term + partner.astype(jnp.float32)).astype(jnp.bfloat16)
        a_refs[b][...] = after
        if b == 0:
            blocks_1.wait()
        p_refs[b][...] = product(t1[b], after).astype(jnp.bfloat16)


def middle_kernel(level, nodes, place, next_place, a_ref, in_ref, t_ref, a_out, p_out):
    own = own_bit(*place)
    other = 1 - own_bit(*next_place)
    for at, node in enumerate(nodes):
        own_term = product(t_ref[level, node, own], a_ref[at])
        after = (own_term + in_ref[at].astype(jnp.float32)).astype(jnp.bfloat16)
        a_out[at] = after
        p_out[at] = product(t_ref[level + 1, node, other], after).astype(jnp.bfloat16)


def last_kernel(level, nodes, start, width, place, a_ref, in_ref, t_ref, *refs):
    out_hbm, out, sems = refs[-3:]
    own = own_bit(*place)
    stores = []
    for at, node in enumerate(nodes):
        own_term = product(t_ref[level, node, own], a_ref[at])
        out[at] = (own_term + in_ref[at].astype(jnp.float32)).astype(jnp.bfloat16)
        stores.append(
            pltpu.make_async_copy(
                out.at[at], out_hbm.at[node, :, :, pl.ds(start, width)], sems.at[at]
            )
        )
        stores[at].start()
    for store in stores:
        store.wait()


def local(inputs, leaf_maps, transfer_blocks):
    nodes, _, rank, rows = leaf_maps.shape
    columns = inputs.shape[3]
    src_bits = lax.axis_size("src").bit_length() - 1
    tgt_bits = lax.axis_size("tgt").bit_length() - 1
    places = [None, ("src", src_bits - 1), ("src", src_bits - 2), ("tgt", tgt_bits - 1)]
    everyone = tuple(range(nodes))
    widths = [width for width, _ in GROUPS]
    starts = [sum(widths[:group]) for group in range(len(GROUPS))]
    chunks = []
    for group, (_, apart) in enumerate(GROUPS):
        chunks += [(group, (node,)) for node in everyone] if apart else [(group, everyone)]

    anywhere = pl.BlockSpec(memory_space=pltpu.HBM)
    here = pl.BlockSpec(memory_space=pltpu.VMEM)
    in_hbm = [
        pltpu.with_memory_space_constraint(array, pltpu.HBM)
        for array in (inputs, leaf_maps, transfer_blocks)
    ]
    cost = pl.CostEstimate(flops=2, bytes_accessed=2, transcendentals=0)

    def params(limit):
        return pltpu.CompilerParams(vmem_limit_bytes=limit)

    def part(group, some):
        return jax.ShapeDtypeStruct((len(some), 2, rank, widths[group]), jnp.bfloat16)

    def leaf(group):
        width, apart = GROUPS[group]
        mine = [some for at, some in chunks if at == group]
        return pl.pallas_call(
            functools.partial(leaf_kernel, starts[group], width, apart, places[1]),
            out_shape=tuple(part(group, some) for some in mine) * 2,
            in_specs=[anywhere] * 3,
            out_specs=(here,) * (2 * len(mine)),
            scratch_shapes=[
                pltpu.VMEM((nodes, 2, rows, width), jnp.bfloat16),
                pltpu.VMEM((nodes, 2, rank, rows), jnp.bfloat16),
                pltpu.VMEM((nodes, 2, 2, rank, rank), jnp.bfloat16),
                pltpu.VMEM((nodes, 2, rank, rank), jnp.bfloat16),
                pltpu.SemaphoreType.DMA((2 * nodes + 2,)),
            ],
            compiler_params=params(LEAF_LIMIT),
            cost_estimate=cost,
            name="leaf",
        )(*in_hbm)

    def middle(level, chunk, held, arrived):
        group, some = chunk
        return pl.pallas_call(
            functools.partial(middle_kernel, level, some, places[level], places[level + 1]),
            out_shape=(part(group, some),) * 2,
            in_specs=[here] * 3,
            out_specs=(here, here),
            compiler_params=params(LIMIT),
            cost_estimate=cost,
            name="middle",
        )(held, arrived, transfer_blocks)

    def last(level, chunk, held, arrived, result):
        group, some = chunk
        operands = (held, arrived, transfer_blocks)
        aliases = {}
        if result is not None:
            operands += (result,)
            aliases = {3: 0}
        return pl.pallas_call(
            functools.partial(
                last_kernel, level, some, starts[group], widths[group], places[level]
            ),
            out_shape=jax.ShapeDtypeStruct((nodes, 2, rank, columns), jnp.bfloat16),
            in_specs=[here] * 3 + [anywhere] * len(aliases),
            out_specs=anywhere,
            scratch_shapes=[
                pltpu.VMEM((len(some), 2, rank, widths[group]), jnp.bfloat16),
                pltpu.SemaphoreType.DMA((len(some),)),
            ],
            input_output_aliases=aliases,
            compiler_params=params(LIMIT),
            cost_estimate=cost,
            name="last",
        )(*operands)

    held, flying = {}, {}
    for group in range(len(GROUPS)):
        mine = [chunk for chunk in chunks if chunk[0] == group]
        results = leaf(group)
        for at, chunk in enumerate(mine):
            held[chunk] = results[at]
            flying[chunk] = partner_2(results[len(mine) + at], *places[1])
    for level in (1, 2):
        for chunk in chunks:
            held[chunk], term = middle(level, chunk, held[chunk], flying[chunk])
            flying[chunk] = partner_2(term, *places[level + 1])
    result = None
    for chunk in chunks:
        result = last(3, chunk, held[chunk], flying[chunk], result)
    return result


def solution(mesh):
    placed = (
        P(("src", "tgt"), None, None, None),
        P(("src", "tgt"), None, None, None),
        P(None, ("src", "tgt"), None, None, None, None),
    )
    return jax.shard_map(
        local,
        mesh=mesh,
        in_specs=placed,
        out_specs=P(("src", "tgt"), None, None, None),
        check_vma=False,
    )
```

```python
import functools

import jax
import jax.numpy as jnp
from jax import lax
from jax.experimental import pallas as pl
from jax.experimental.pallas import tpu as pltpu
from jax.sharding import PartitionSpec as P

GROUPS = ((128, False), (128, False), (128, False), (128, False))
LEAF_LIMIT = 24 * 1024 * 1024
LIMIT = 16 * 1024 * 1024


def partner_2(block, axis, apart):
    count = lax.axis_size(axis)
    route = []
    for low in range(count):
        high = low | 1 << apart
        if high != low and high < count:
            route += [(low, high), (high, low)]
    return lax.ppermute(block, axis, route)


def own_bit(axis, place):
    return lax.rem(lax.div(lax.axis_index(axis), 2**place), 2)


def product(blocks, vectors):
    rank, width = blocks.shape[1], vectors.shape[2]
    if width >= 256:
        stacked = vectors.reshape(2 * vectors.shape[1], width)
        real_rows = jnp.concatenate([blocks[0], -blocks[1]], axis=1)
        imag_rows = jnp.concatenate([blocks[1], blocks[0]], axis=1)
        rows = jnp.concatenate([real_rows, imag_rows], axis=0)
        both = jnp.dot(rows, stacked, preferred_element_type=jnp.float32)
        return both.reshape(2, rank, width)
    rows = blocks.reshape(2 * rank, blocks.shape[2])
    beside = jnp.concatenate([vectors[0], vectors[1]], axis=1)
    all_four = jnp.dot(rows, beside, preferred_element_type=jnp.float32)
    real_part = all_four[:rank, :width] - all_four[rank:, width:]
    imag_part = all_four[:rank, width:] + all_four[rank:, :width]
    return jnp.stack([real_part, imag_part])


def leaf_kernel(start, width, apart, place, x_hbm, l_hbm, t_hbm, *refs):
    nodes = l_hbm.shape[0]
    outs, (x, l, t0, t1, sems) = refs[:-5], refs[-5:]
    if apart:
        a_refs, p_refs = [ref.at[0] for ref in outs[:nodes]], [ref.at[0] for ref in outs[nodes:]]
    else:
        a_refs, p_refs = [[ref.at[b] for b in range(nodes)] for ref in outs]
    other = 1 - own_bit(*place)
    columns = pl.ds(start, width)
    moves = []
    for b in range(nodes):
        moves.append(
            (
                pltpu.make_async_copy(x_hbm.at[b, :, :, columns], x.at[b], sems.at[2 * b]),
                pltpu.make_async_copy(l_hbm.at[b], l.at[b], sems.at[2 * b + 1]),
            )
        )
    blocks_0 = pltpu.make_async_copy(t_hbm.at[0], t0, sems.at[2 * nodes])
    blocks_1 = pltpu.make_async_copy(t_hbm.at[1, :, other], t1, sems.at[2 * nodes + 1])
    for pair in moves:
        for move in pair:
            move.start()
    blocks_0.start()
    blocks_1.start()
    coeffs = []
    for b in range(nodes):
        for move in moves[b]:
            move.wait()
        coeffs.append(product(l[b], x[b]).astype(jnp.bfloat16))
    blocks_0.wait()
    for b in range(nodes):
        own_term = product(t0[b, b], coeffs[b])
        partner = product(t0[1 - b, b], coeffs[1 - b]).astype(jnp.bfloat16)
        after = (own_term + partner.astype(jnp.float32)).astype(jnp.bfloat16)
        a_refs[b][...] = after
        if b == 0:
            blocks_1.wait()
        p_refs[b][...] = product(t1[b], after).astype(jnp.bfloat16)


def own_kernel(level, nodes, place, a_ref, t_ref, own_ref):
    own = own_bit(*place)
    for at, node in enumerate(nodes):
        own_ref[at] = product(t_ref[level, node, own], a_ref[at])


def own_term_of(held, t_ref, level, at, node, place):
    if held.dtype == jnp.float32:
        return held[at]
    return product(t_ref[level, node, own_bit(*place)], held[at])


def middle_kernel(level, nodes, place, next_place, a_ref, in_ref, t_ref, a_out, p_out):
    other = 1 - own_bit(*next_place)
    for at, node in enumerate(nodes):
        own_term = own_term_of(a_ref, t_ref, level, at, node, place)
        after = (own_term + in_ref[at].astype(jnp.float32)).astype(jnp.bfloat16)
        a_out[at] = after
        p_out[at] = product(t_ref[level + 1, node, other], after).astype(jnp.bfloat16)


def last_kernel(level, nodes, start, width, place, a_ref, in_ref, t_ref, *refs):
    out_hbm, out, sems = refs[-3:]
    stores = []
    for at, node in enumerate(nodes):
        own_term = own_term_of(a_ref, t_ref, level, at, node, place)
        out[at] = (own_term + in_ref[at].astype(jnp.float32)).astype(jnp.bfloat16)
        stores.append(
            pltpu.make_async_copy(
                out.at[at], out_hbm.at[node, :, :, pl.ds(start, width)], sems.at[at]
            )
        )
        stores[at].start()
    for store in stores:
        store.wait()


def local(inputs, leaf_maps, transfer_blocks):
    nodes, _, rank, rows = leaf_maps.shape
    columns = inputs.shape[3]
    src_bits = lax.axis_size("src").bit_length() - 1
    tgt_bits = lax.axis_size("tgt").bit_length() - 1
    places = [None, ("src", src_bits - 1), ("src", src_bits - 2), ("tgt", tgt_bits - 1)]
    everyone = tuple(range(nodes))
    widths = [width for width, _ in GROUPS]
    starts = [sum(widths[:group]) for group in range(len(GROUPS))]
    chunks = []
    for group, (_, apart) in enumerate(GROUPS):
        chunks += [(group, (node,)) for node in everyone] if apart else [(group, everyone)]

    anywhere = pl.BlockSpec(memory_space=pltpu.HBM)
    here = pl.BlockSpec(memory_space=pltpu.VMEM)
    in_hbm = [
        pltpu.with_memory_space_constraint(array, pltpu.HBM)
        for array in (inputs, leaf_maps, transfer_blocks)
    ]
    cost = pl.CostEstimate(flops=2, bytes_accessed=2, transcendentals=0)

    def params(limit):
        return pltpu.CompilerParams(vmem_limit_bytes=limit)

    def part(group, some):
        return jax.ShapeDtypeStruct((len(some), 2, rank, widths[group]), jnp.bfloat16)

    def leaf(group):
        width, apart = GROUPS[group]
        mine = [some for at, some in chunks if at == group]
        return pl.pallas_call(
            functools.partial(leaf_kernel, starts[group], width, apart, places[1]),
            out_shape=tuple(part(group, some) for some in mine) * 2,
            in_specs=[anywhere] * 3,
            out_specs=(here,) * (2 * len(mine)),
            scratch_shapes=[
                pltpu.VMEM((nodes, 2, rows, width), jnp.bfloat16),
                pltpu.VMEM((nodes, 2, rank, rows), jnp.bfloat16),
                pltpu.VMEM((nodes, 2, 2, rank, rank), jnp.bfloat16),
                pltpu.VMEM((nodes, 2, rank, rank), jnp.bfloat16),
                pltpu.SemaphoreType.DMA((2 * nodes + 2,)),
            ],
            compiler_params=params(LEAF_LIMIT),
            cost_estimate=cost,
            name="leaf",
        )(*in_hbm)

    def own(level, chunk, held):
        group, some = chunk
        return pl.pallas_call(
            functools.partial(own_kernel, level, some, places[level]),
            out_shape=jax.ShapeDtypeStruct((len(some), 2, rank, widths[group]), jnp.float32),
            in_specs=[here] * 2,
            out_specs=here,
            compiler_params=params(LIMIT),
            cost_estimate=cost,
            name="own",
        )(held, transfer_blocks)

    def middle(level, chunk, held, arrived):
        group, some = chunk
        return pl.pallas_call(
            functools.partial(middle_kernel, level, some, places[level], places[level + 1]),
            out_shape=(part(group, some),) * 2,
            in_specs=[here] * 3,
            out_specs=(here, here),
            compiler_params=params(LIMIT),
            cost_estimate=cost,
            name="middle",
        )(held, arrived, transfer_blocks)

    def last(level, chunk, held, arrived, result):
        group, some = chunk
        operands = (held, arrived, transfer_blocks)
        aliases = {}
        if result is not None:
            operands += (result,)
            aliases = {3: 0}
        return pl.pallas_call(
            functools.partial(
                last_kernel, level, some, starts[group], widths[group], places[level]
            ),
            out_shape=jax.ShapeDtypeStruct((nodes, 2, rank, columns), jnp.bfloat16),
            in_specs=[here] * 3 + [anywhere] * len(aliases),
            out_specs=anywhere,
            scratch_shapes=[
                pltpu.VMEM((len(some), 2, rank, widths[group]), jnp.bfloat16),
                pltpu.SemaphoreType.DMA((len(some),)),
            ],
            input_output_aliases=aliases,
            compiler_params=params(LIMIT),
            cost_estimate=cost,
            name="last",
        )(*operands)

    held, flying = {}, {}
    for group in range(len(GROUPS)):
        mine = [chunk for chunk in chunks if chunk[0] == group]
        results = leaf(group)
        for at, chunk in enumerate(mine):
            held[chunk] = results[at]
            flying[chunk] = partner_2(results[len(mine) + at], *places[1])
    for level in (1, 2):
        for chunk in chunks:
            held[chunk], term = middle(level, chunk, held[chunk], flying[chunk])
            flying[chunk] = partner_2(term, *places[level + 1])
            held[chunk] = own(level + 1, chunk, held[chunk])
    result = None
    for chunk in chunks:
        result = last(3, chunk, held[chunk], flying[chunk], result)
    return result


def solution(mesh):
    placed = (
        P(("src", "tgt"), None, None, None),
        P(("src", "tgt"), None, None, None),
        P(None, ("src", "tgt"), None, None, None, None),
    )
    return jax.shard_map(
        local,
        mesh=mesh,
        in_specs=placed,
        out_specs=P(("src", "tgt"), None, None, None),
        check_vma=False,
    )
```

```python
import functools

import jax
import jax.numpy as jnp
from jax import lax
from jax.experimental import pallas as pl
from jax.experimental.pallas import tpu as pltpu
from jax.sharding import PartitionSpec as P

GROUPS = ((128, False), (128, False), (256, True))
LEAF_LIMIT = 24 * 1024 * 1024
LIMIT = 16 * 1024 * 1024


def partner_2(block, axis, apart):
    count = lax.axis_size(axis)
    route = []
    for low in range(count):
        high = low | 1 << apart
        if high != low and high < count:
            route += [(low, high), (high, low)]
    return lax.ppermute(block, axis, route)


def own_bit(axis, place):
    return lax.rem(lax.div(lax.axis_index(axis), 2**place), 2)


def product(blocks, vectors):
    rank, width = blocks.shape[1], vectors.shape[2]
    if width >= 256:
        stacked = vectors.reshape(2 * vectors.shape[1], width)
        real_rows = jnp.concatenate([blocks[0], -blocks[1]], axis=1)
        imag_rows = jnp.concatenate([blocks[1], blocks[0]], axis=1)
        rows = jnp.concatenate([real_rows, imag_rows], axis=0)
        both = jnp.dot(rows, stacked, preferred_element_type=jnp.float32)
        return both.reshape(2, rank, width)
    rows = blocks.reshape(2 * rank, blocks.shape[2])
    beside = jnp.concatenate([vectors[0], vectors[1]], axis=1)
    all_four = jnp.dot(rows, beside, preferred_element_type=jnp.float32)
    real_part = all_four[:rank, :width] - all_four[rank:, width:]
    imag_part = all_four[:rank, width:] + all_four[rank:, :width]
    return jnp.stack([real_part, imag_part])


def leaf_kernel(start, width, apart, place, gates, x_hbm, l_hbm, t_hbm, *refs):
    refs = refs[gates:]
    nodes = l_hbm.shape[0]
    outs, (x, l, t0, t1, sems) = refs[:-5], refs[-5:]
    if apart:
        a_refs, p_refs = [ref.at[0] for ref in outs[:nodes]], [ref.at[0] for ref in outs[nodes:]]
    else:
        a_refs, p_refs = [[ref.at[b] for b in range(nodes)] for ref in outs]
    other = 1 - own_bit(*place)
    columns = pl.ds(start, width)
    moves = []
    for b in range(nodes):
        moves.append(
            (
                pltpu.make_async_copy(x_hbm.at[b, :, :, columns], x.at[b], sems.at[2 * b]),
                pltpu.make_async_copy(l_hbm.at[b], l.at[b], sems.at[2 * b + 1]),
            )
        )
    blocks_0 = pltpu.make_async_copy(t_hbm.at[0], t0, sems.at[2 * nodes])
    blocks_1 = pltpu.make_async_copy(t_hbm.at[1, :, other], t1, sems.at[2 * nodes + 1])
    for pair in moves:
        for move in pair:
            move.start()
    blocks_0.start()
    blocks_1.start()
    coeffs = []
    for b in range(nodes):
        for move in moves[b]:
            move.wait()
        coeffs.append(product(l[b], x[b]).astype(jnp.bfloat16))
    blocks_0.wait()
    for b in range(nodes):
        own_term = product(t0[b, b], coeffs[b])
        partner = product(t0[1 - b, b], coeffs[1 - b]).astype(jnp.bfloat16)
        after = (own_term + partner.astype(jnp.float32)).astype(jnp.bfloat16)
        a_refs[b][...] = after
        if b == 0:
            blocks_1.wait()
        p_refs[b][...] = product(t1[b], after).astype(jnp.bfloat16)


def own_kernel(level, nodes, place, a_ref, t_ref, own_ref):
    own = own_bit(*place)
    for at, node in enumerate(nodes):
        own_ref[at] = product(t_ref[level, node, own], a_ref[at])


def own_term_of(held, t_ref, level, at, node, place):
    if held.dtype == jnp.float32:
        return held[at]
    return product(t_ref[level, node, own_bit(*place)], held[at])


def middle_kernel(level, nodes, place, next_place, a_ref, in_ref, t_ref, a_out, p_out):
    other = 1 - own_bit(*next_place)
    for at, node in enumerate(nodes):
        own_term = own_term_of(a_ref, t_ref, level, at, node, place)
        after = (own_term + in_ref[at].astype(jnp.float32)).astype(jnp.bfloat16)
        a_out[at] = after
        p_out[at] = product(t_ref[level + 1, node, other], after).astype(jnp.bfloat16)


def last_kernel(level, nodes, start, width, place, a_ref, in_ref, t_ref, *refs):
    out_hbm, out, sems = refs[-3:]
    stores = []
    for at, node in enumerate(nodes):
        own_term = own_term_of(a_ref, t_ref, level, at, node, place)
        out[at] = (own_term + in_ref[at].astype(jnp.float32)).astype(jnp.bfloat16)
        stores.append(
            pltpu.make_async_copy(
                out.at[at], out_hbm.at[node, :, :, pl.ds(start, width)], sems.at[at]
            )
        )
        stores[at].start()
    for store in stores:
        store.wait()


def local(inputs, leaf_maps, transfer_blocks):
    nodes, _, rank, rows = leaf_maps.shape
    columns = inputs.shape[3]
    src_bits = lax.axis_size("src").bit_length() - 1
    tgt_bits = lax.axis_size("tgt").bit_length() - 1
    places = [None, ("src", src_bits - 1), ("src", src_bits - 2), ("tgt", tgt_bits - 1)]
    everyone = tuple(range(nodes))
    widths = [width for width, _ in GROUPS]
    starts = [sum(widths[:group]) for group in range(len(GROUPS))]
    chunks = []
    for group, (_, apart) in enumerate(GROUPS):
        chunks += [(group, (node,)) for node in everyone] if apart else [(group, everyone)]

    anywhere = pl.BlockSpec(memory_space=pltpu.HBM)
    here = pl.BlockSpec(memory_space=pltpu.VMEM)
    in_hbm = [
        pltpu.with_memory_space_constraint(array, pltpu.HBM)
        for array in (inputs, leaf_maps, transfer_blocks)
    ]
    cost = pl.CostEstimate(flops=2, bytes_accessed=2, transcendentals=0)

    def params(limit):
        return pltpu.CompilerParams(vmem_limit_bytes=limit)

    def part(group, some):
        return jax.ShapeDtypeStruct((len(some), 2, rank, widths[group]), jnp.bfloat16)

    def leaf(group, gates):
        width, apart = GROUPS[group]
        mine = [some for at, some in chunks if at == group]
        return pl.pallas_call(
            functools.partial(leaf_kernel, starts[group], width, apart, places[1], len(gates)),
            out_shape=tuple(part(group, some) for some in mine) * 2,
            in_specs=[anywhere] * 3 + [pl.BlockSpec(memory_space=pl.ANY)] * len(gates),
            out_specs=(here,) * (2 * len(mine)),
            scratch_shapes=[
                pltpu.VMEM((nodes, 2, rows, width), jnp.bfloat16),
                pltpu.VMEM((nodes, 2, rank, rows), jnp.bfloat16),
                pltpu.VMEM((nodes, 2, 2, rank, rank), jnp.bfloat16),
                pltpu.VMEM((nodes, 2, rank, rank), jnp.bfloat16),
                pltpu.SemaphoreType.DMA((2 * nodes + 2,)),
            ],
            compiler_params=params(LEAF_LIMIT),
            cost_estimate=cost,
            name="leaf",
        )(*in_hbm, *gates)

    def own(level, chunk, held):
        group, some = chunk
        return pl.pallas_call(
            functools.partial(own_kernel, level, some, places[level]),
            out_shape=jax.ShapeDtypeStruct((len(some), 2, rank, widths[group]), jnp.float32),
            in_specs=[here] * 2,
            out_specs=here,
            compiler_params=params(LIMIT),
            cost_estimate=cost,
            name="own",
        )(held, transfer_blocks)

    def middle(level, chunk, held, arrived):
        group, some = chunk
        return pl.pallas_call(
            functools.partial(middle_kernel, level, some, places[level], places[level + 1]),
            out_shape=(part(group, some),) * 2,
            in_specs=[here] * 3,
            out_specs=(here, here),
            compiler_params=params(LIMIT),
            cost_estimate=cost,
            name="middle",
        )(held, arrived, transfer_blocks)

    def last(level, chunk, held, arrived, result):
        group, some = chunk
        operands = (held, arrived, transfer_blocks)
        aliases = {}
        if result is not None:
            operands += (result,)
            aliases = {3: 0}
        return pl.pallas_call(
            functools.partial(
                last_kernel, level, some, starts[group], widths[group], places[level]
            ),
            out_shape=jax.ShapeDtypeStruct((nodes, 2, rank, columns), jnp.bfloat16),
            in_specs=[here] * 3 + [anywhere] * len(aliases),
            out_specs=anywhere,
            scratch_shapes=[
                pltpu.VMEM((len(some), 2, rank, widths[group]), jnp.bfloat16),
                pltpu.SemaphoreType.DMA((len(some),)),
            ],
            input_output_aliases=aliases,
            compiler_params=params(LIMIT),
            cost_estimate=cost,
            name="last",
        )(*operands)

    held, flying, gates = {}, {}, ()
    for group in range(len(GROUPS)):
        mine = [chunk for chunk in chunks if chunk[0] == group]
        results = leaf(group, gates)
        gates = results[:1]
        for at, chunk in enumerate(mine):
            held[chunk] = results[at]
            flying[chunk] = partner_2(results[len(mine) + at], *places[1])
    for level in (1, 2):
        for chunk in chunks:
            held[chunk], term = middle(level, chunk, held[chunk], flying[chunk])
            flying[chunk] = partner_2(term, *places[level + 1])
            held[chunk] = own(level + 1, chunk, held[chunk])
    result = None
    for chunk in chunks:
        result = last(3, chunk, held[chunk], flying[chunk], result)
    return result


def solution(mesh):
    placed = (
        P(("src", "tgt"), None, None, None),
        P(("src", "tgt"), None, None, None),
        P(None, ("src", "tgt"), None, None, None, None),
    )
    return jax.shard_map(
        local,
        mesh=mesh,
        in_specs=placed,
        out_specs=P(("src", "tgt"), None, None, None),
        check_vma=False,
    )
```

```python
import functools

import jax
import jax.numpy as jnp
from jax import lax
from jax.experimental import pallas as pl
from jax.experimental.pallas import tpu as pltpu
from jax.sharding import PartitionSpec as P

GROUPS = ((128, False), (128, False), (128, False), (128, False))
LEAF_LIMIT = 24 * 1024 * 1024
LIMIT = 16 * 1024 * 1024


def partner_2(block, axis, apart):
    count = lax.axis_size(axis)
    route = []
    for low in range(count):
        high = low | 1 << apart
        if high != low and high < count:
            route += [(low, high), (high, low)]
    return lax.ppermute(block, axis, route)


def own_bit(axis, place):
    return lax.rem(lax.div(lax.axis_index(axis), 2**place), 2)


def product(blocks, vectors):
    rank, width = blocks.shape[1], vectors.shape[2]
    if width >= 256:
        stacked = vectors.reshape(2 * vectors.shape[1], width)
        real_rows = jnp.concatenate([blocks[0], -blocks[1]], axis=1)
        imag_rows = jnp.concatenate([blocks[1], blocks[0]], axis=1)
        rows = jnp.concatenate([real_rows, imag_rows], axis=0)
        both = jnp.dot(rows, stacked, preferred_element_type=jnp.float32)
        return both.reshape(2, rank, width)
    rows = blocks.reshape(2 * rank, blocks.shape[2])
    beside = jnp.concatenate([vectors[0], vectors[1]], axis=1)
    all_four = jnp.dot(rows, beside, preferred_element_type=jnp.float32)
    real_part = all_four[:rank, :width] - all_four[rank:, width:]
    imag_part = all_four[:rank, width:] + all_four[rank:, :width]
    return jnp.stack([real_part, imag_part])


def leaf_kernel(start, width, apart, place, x_hbm, l_hbm, t_hbm, *refs):
    nodes = l_hbm.shape[0]
    outs, (x, l, t0, t1, sems) = refs[:-5], refs[-5:]
    if apart:
        a_refs, p_refs = [ref.at[0] for ref in outs[:nodes]], [ref.at[0] for ref in outs[nodes:]]
    else:
        a_refs, p_refs = [[ref.at[b] for b in range(nodes)] for ref in outs]
    other = 1 - own_bit(*place)
    columns = pl.ds(start, width)
    moves = []
    for b in range(nodes):
        moves.append(
            (
                pltpu.make_async_copy(x_hbm.at[b, :, :, columns], x.at[b], sems.at[2 * b]),
                pltpu.make_async_copy(l_hbm.at[b], l.at[b], sems.at[2 * b + 1]),
            )
        )
    blocks_0 = pltpu.make_async_copy(t_hbm.at[0], t0, sems.at[2 * nodes])
    blocks_1 = pltpu.make_async_copy(t_hbm.at[1, :, other], t1, sems.at[2 * nodes + 1])
    for pair in moves:
        for move in pair:
            move.start()
    blocks_0.start()
    blocks_1.start()
    coeffs = []
    for b in range(nodes):
        for move in moves[b]:
            move.wait()
        coeffs.append(product(l[b], x[b]).astype(jnp.bfloat16))
    blocks_0.wait()
    for b in range(nodes):
        own_term = product(t0[b, b], coeffs[b])
        partner = product(t0[1 - b, b], coeffs[1 - b]).astype(jnp.bfloat16)
        after = (own_term + partner.astype(jnp.float32)).astype(jnp.bfloat16)
        a_refs[b][...] = after
        if b == 0:
            blocks_1.wait()
        p_refs[b][...] = product(t1[b], after).astype(jnp.bfloat16)


def own_kernel(level, nodes, place, a_ref, t_ref, own_ref):
    own = own_bit(*place)
    for at, node in enumerate(nodes):
        own_ref[at] = product(t_ref[level, node, own], a_ref[at])


def own_term_of(held, t_ref, level, at, node, place):
    if held.dtype == jnp.float32:
        return held[at]
    return product(t_ref[level, node, own_bit(*place)], held[at])


def middle_kernel(level, nodes, place, next_place, a_ref, in_ref, t_ref, a_out, p_out):
    other = 1 - own_bit(*next_place)
    for at, node in enumerate(nodes):
        own_term = own_term_of(a_ref, t_ref, level, at, node, place)
        after = (own_term + in_ref[at].astype(jnp.float32)).astype(jnp.bfloat16)
        a_out[at] = after
        p_out[at] = product(t_ref[level + 1, node, other], after).astype(jnp.bfloat16)


def last_kernel(level, nodes, start, width, place, a_ref, in_ref, t_ref, *refs):
    out_hbm, out, sems = refs[-3:]
    stores = []
    for at, node in enumerate(nodes):
        own_term = own_term_of(a_ref, t_ref, level, at, node, place)
        out[at] = (own_term + in_ref[at].astype(jnp.float32)).astype(jnp.bfloat16)
        stores.append(
            pltpu.make_async_copy(
                out.at[at], out_hbm.at[node, :, :, pl.ds(start, width)], sems.at[at]
            )
        )
        stores[at].start()
    for store in stores:
        store.wait()


def local(inputs, leaf_maps, transfer_blocks):
    nodes, _, rank, rows = leaf_maps.shape
    columns = inputs.shape[3]
    src_bits = lax.axis_size("src").bit_length() - 1
    tgt_bits = lax.axis_size("tgt").bit_length() - 1
    places = [None, ("src", src_bits - 1), ("src", src_bits - 2), ("tgt", tgt_bits - 1)]
    everyone = tuple(range(nodes))
    widths = [width for width, _ in GROUPS]
    starts = [sum(widths[:group]) for group in range(len(GROUPS))]
    chunks = []
    for group, (_, apart) in enumerate(GROUPS):
        chunks += [(group, (node,)) for node in everyone] if apart else [(group, everyone)]

    anywhere = pl.BlockSpec(memory_space=pltpu.HBM)
    here = pl.BlockSpec(memory_space=pltpu.VMEM)
    in_hbm = [
        pltpu.with_memory_space_constraint(array, pltpu.HBM)
        for array in (inputs, leaf_maps, transfer_blocks)
    ]
    cost = pl.CostEstimate(flops=2, bytes_accessed=2, transcendentals=0)

    def params(limit):
        return pltpu.CompilerParams(vmem_limit_bytes=limit)

    def part(group, some):
        return jax.ShapeDtypeStruct((len(some), 2, rank, widths[group]), jnp.bfloat16)

    def leaf(group):
        width, apart = GROUPS[group]
        mine = [some for at, some in chunks if at == group]
        return pl.pallas_call(
            functools.partial(leaf_kernel, starts[group], width, apart, places[1]),
            out_shape=tuple(part(group, some) for some in mine) * 2,
            in_specs=[anywhere] * 3,
            out_specs=(here,) * (2 * len(mine)),
            scratch_shapes=[
                pltpu.VMEM((nodes, 2, rows, width), jnp.bfloat16),
                pltpu.VMEM((nodes, 2, rank, rows), jnp.bfloat16),
                pltpu.VMEM((nodes, 2, 2, rank, rank), jnp.bfloat16),
                pltpu.VMEM((nodes, 2, rank, rank), jnp.bfloat16),
                pltpu.SemaphoreType.DMA((2 * nodes + 2,)),
            ],
            compiler_params=params(LEAF_LIMIT),
            cost_estimate=cost,
            name="leaf",
        )(*in_hbm)

    def own(level, chunk, held):
        group, some = chunk
        return pl.pallas_call(
            functools.partial(own_kernel, level, some, places[level]),
            out_shape=jax.ShapeDtypeStruct((len(some), 2, rank, widths[group]), jnp.float32),
            in_specs=[here] * 2,
            out_specs=here,
            compiler_params=params(LIMIT),
            cost_estimate=cost,
            name="own",
        )(held, transfer_blocks)

    def middle(level, chunk, held, arrived):
        group, some = chunk
        return pl.pallas_call(
            functools.partial(middle_kernel, level, some, places[level], places[level + 1]),
            out_shape=(part(group, some),) * 2,
            in_specs=[here] * 3,
            out_specs=(here, here),
            compiler_params=params(LIMIT),
            cost_estimate=cost,
            name="middle",
        )(held, arrived, transfer_blocks)

    def last(level, chunk, held, arrived, result):
        group, some = chunk
        operands = (held, arrived, transfer_blocks)
        aliases = {}
        if result is not None:
            operands += (result,)
            aliases = {3: 0}
        return pl.pallas_call(
            functools.partial(
                last_kernel, level, some, starts[group], widths[group], places[level]
            ),
            out_shape=jax.ShapeDtypeStruct((nodes, 2, rank, columns), jnp.bfloat16),
            in_specs=[here] * 3 + [anywhere] * len(aliases),
            out_specs=anywhere,
            scratch_shapes=[
                pltpu.VMEM((len(some), 2, rank, widths[group]), jnp.bfloat16),
                pltpu.SemaphoreType.DMA((len(some),)),
            ],
            input_output_aliases=aliases,
            compiler_params=params(LIMIT),
            cost_estimate=cost,
            name="last",
        )(*operands)

    held, flying = {}, {}
    for group in range(len(GROUPS)):
        mine = [chunk for chunk in chunks if chunk[0] == group]
        results = leaf(group)
        for at, chunk in enumerate(mine):
            flying[chunk] = partner_2(results[len(mine) + at], *places[1])
            held[chunk] = own(1, chunk, results[at])
    for level in (1, 2):
        for chunk in chunks:
            held[chunk], term = middle(level, chunk, held[chunk], flying[chunk])
            flying[chunk] = partner_2(term, *places[level + 1])
            held[chunk] = own(level + 1, chunk, held[chunk])
    result = None
    for chunk in chunks:
        result = last(3, chunk, held[chunk], flying[chunk], result)
    return result


def solution(mesh):
    placed = (
        P(("src", "tgt"), None, None, None),
        P(("src", "tgt"), None, None, None),
        P(None, ("src", "tgt"), None, None, None, None),
    )
    return jax.shard_map(
        local,
        mesh=mesh,
        in_specs=placed,
        out_specs=P(("src", "tgt"), None, None, None),
        check_vma=False,
    )
```
